32 devices in a mesh: grid: 4 (over z), elec: 8 (over y, x, core).
Axes of the slice: x: 2, y: 2, z: 4, core: 2. Of those that a mesh axis runs over, the one named last changes fastest.
Arguments:
- electric: bfloat16 [2, 8192, 8192], P(None, 'elec', 'grid'), may hold values from -6 to 6
- trial: bfloat16 [8192, 2, 128], P('grid'), may hold values from -0.0625 to 0.0625
- counts: int32 [8], replicated, may hold values from 1 to 1024, as said below
Outputs:
- field: float32 [8192, 2, 128], P(('grid', 'elec'))
The draws below stay inside these ranges and needn't reach their ends.
Inputs may be any that keep to these rules, and one draw needn't show every extreme that they name: `counts`: at least one group holds exactly 1024 live electrons.
All inputs are finite; a program needn't handle non-finite values.
Results may differ from the reference program's by a relative error of at most 0.0023.
Values sent between devices are 32-bit elements; how exact they have to be, the bound alone decides.
A program may use at most 64 MiB of HBM per device.

```python
import jax
import jax.numpy as jnp
from jax import lax

MODES = 128
CAP = 1024
GROUPS = 8
SLOTS = 8192
GRID = 8192


def draw_counts(key, part):
    base = jax.random.fold_in(key, 11)
    first_key, second_key, third_key = jax.random.split(base, 3)
    first_pick = jax.random.randint(first_key, (GROUPS,), 0, CAP)
    second_pick = jax.random.randint(second_key, (GROUPS,), 0, CAP)
    skewed = 1 + first_pick * second_pick // CAP
    fullest = jax.random.randint(third_key, (), 0, GROUPS)
    positions = jnp.arange(GROUPS, dtype=jnp.int32)
    return jnp.where(positions == fullest, CAP, skewed).astype(jnp.int32)


def block_levels(key, dims, shards, low, high):
    def one(dim, shards_of):
        heights = jax.random.uniform(jax.random.fold_in(jax.random.fold_in(key, 6), dim), (shards_of,), jnp.float32, low / len(shards), high / len(shards))
        return jnp.repeat(jnp.exp(heights), dims[dim] // shards_of).reshape((-1,) + (1,) * (len(dims) - dim - 1))

    factor_of = one(*shards[0])
    for cut in shards[1:]:
        factor_of = factor_of * one(*cut)
    return factor_of


def scatter_about(own_key, shape, spread, reach, shards=(), kind=jnp.bfloat16):
    entries = jax.random.normal(own_key, shape, jnp.float32) * spread
    if len(shards) > 0:
        entries = block_levels(own_key, shape, shards, -0.22, 0.18) * entries
    return jnp.clip(entries, min=-reach, max=reach).astype(kind)


def setup_inputs(seed: int = 0) -> dict:
    keys = jax.random.split(jax.random.key(seed), 4)
    return {
        "electric": scatter_about(keys[0], (2, SLOTS, GRID), 1.0, 6.0, ((1, 8), (2, 4))),
        "trial": scatter_about(keys[1], (GRID, 2, MODES), GRID ** -0.5, 0.0625, ((0, 4),)),
        "counts": draw_counts(jax.random.fold_in(keys[3], 71), 0),
    }


def reference(electric, trial, counts):
    groups = counts.shape[0]
    capacity = electric.shape[1] // groups
    points = electric.shape[2]
    mode_count = trial.shape[2]
    trial_flat = trial.reshape(points, 2 * mode_count)
    total_live = jnp.sum(counts.astype(jnp.float32))
    scaling = 1.0 / jnp.sqrt(total_live)
    slot_ids = jnp.arange(capacity, dtype=jnp.int32)

    def add_group(group_idx, running):
        slab = lax.dynamic_slice_in_dim(electric, (group_idx * capacity).astype(jnp.int32), capacity, 1)
        flattened = slab.reshape(2 * capacity, points)
        products = jnp.dot(flattened, trial_flat, preferred_element_type=jnp.float32)
        real_part = products[:capacity, :mode_count] + products[capacity:, mode_count:]
        imag_part = products[:capacity, mode_count:] - products[capacity:, :mode_count]
        live_count = lax.dynamic_slice_in_dim(counts, group_idx.astype(jnp.int32), 1, 0)[0]
        weights = jnp.where(slot_ids < live_count, 1.0, 0.0).astype(jnp.float32) * scaling
        coef_real = (real_part * weights[:, None]).astype(jnp.bfloat16)
        coef_imag = (imag_part * weights[:, None]).astype(jnp.bfloat16)
        coef_matrix = jnp.concatenate([jnp.concatenate([coef_real, coef_imag], 1), jnp.concatenate([-coef_imag, coef_real], 1)], 0)
        partial_value = lax.dot_general(flattened, coef_matrix, (((0,), (0,)), ((), ())), preferred_element_type=jnp.float32)
        return running + partial_value
    result = lax.fori_loop(0, groups, add_group, jnp.zeros((points, 2 * mode_count), jnp.float32))
    return result.reshape(points, 2, mode_count)
```

```python
import functools

import jax
import jax.numpy as jnp
from jax import lax
from jax.experimental import pallas as pl
from jax.experimental.pallas import tpu as pltpu
from jax.sharding import PartitionSpec as P

MESH = pl.DeviceIdType.MESH
HOP = 2


def kernel(
    n, chips, chunks, blocks,
    counts_ref, trial_ref, electric_ref, out_ref,
    ebuf, part, rl, rr, sl, sr, x0, x1, f, r1, g, r2, fin,
    esem, slsem, rlsem, srsem, rrsem, s1s, s1r, s2s, s2r,
):
    cap = ebuf.shape[1]
    points = ebuf.shape[2]
    modes = trial_ref.shape[1]
    mc = modes // chunks
    sl_n = cap // blocks
    pieces = chunks * blocks
    share = f.shape[-1]
    i = lax.axis_index("grid")
    e = lax.axis_index("elec")
    core = lax.rem(e, 2)
    chip = lax.div(e, 2)
    partner = e + 1 - 2 * core

    def load(s, z):
        return pltpu.make_async_copy(
            electric_ref.at[z, pl.ds(s * sl_n, sl_n), :],
            ebuf.at[z, pl.ds(s * sl_n, sl_n), :],
            esem.at[s, z],
        )

    for s in range(blocks):
        load(s, 0).start()
        load(s, 1).start()

    barrier = pltpu.get_barrier_semaphore()

    for d in (1, n - 1):
        pl.semaphore_signal(barrier, inc=1, device_id=(lax.rem(i + d, n), e), device_id_type=MESH)

    pl.semaphore_signal(barrier, inc=1, device_id=(i, partner), device_id_type=MESH)
    for d in range(1, chips):
        q = lax.rem(chip + d, chips)
        pl.semaphore_signal(barrier, inc=1, device_id=(i, 2 * q + core), device_id_type=MESH)

    def right(k, src):
        return pltpu.make_async_remote_copy(
            src_ref=src.at[k], dst_ref=rl.at[k], send_sem=slsem.at[k], recv_sem=rlsem.at[k],
            device_id=(i + 1, e), device_id_type=MESH,
        )

    def left(k, src):
        return pltpu.make_async_remote_copy(
            src_ref=src.at[k], dst_ref=rr.at[k], send_sem=srsem.at[k], recv_sem=rrsem.at[k],
            device_id=(i - 1, e), device_id_type=MESH,
        )

    def send_ends(k):
        @pl.when(i == 0)
        def _():
            right(k, part).start()

        @pl.when(i == n - 1)
        def _():
            left(k, part).start()

    vt = trial_ref[...].reshape(2 * modes, points)
    dims = (((1,), (1,)), ((), ()))
    for s in range(blocks):
        load(s, 0).wait()
        load(s, 1).wait()
        q0 = lax.dot_general(vt, ebuf[0, s * sl_n:(s + 1) * sl_n, :], dims, preferred_element_type=jnp.float32)
        q1 = lax.dot_general(vt, ebuf[1, s * sl_n:(s + 1) * sl_n, :], dims, preferred_element_type=jnp.float32)
        real = q0[:modes] + q1[modes:]
        imag = q0[modes:] - q1[:modes]
        for c in range(chunks):
            part[c * blocks + s, :mc] = real[c * mc:(c + 1) * mc]
            part[c * blocks + s, mc:] = imag[c * mc:(c + 1) * mc]
        if s == 0:
            pl.semaphore_wait(barrier, chips + 2)
        send_ends(s)

    def rest(k, _):
        send_ends(k)
        return 0

    lax.fori_loop(blocks, pieces, rest, 0)

    live = counts_ref[e]
    total_live = lax.fori_loop(0, 2 * chips, lambda j, v: v + counts_ref[j], jnp.int32(0))
    scaling = 1.0 / jnp.sqrt(jnp.full((8, sl_n), total_live, jnp.int32).astype(jnp.float32))
    scaling = scaling[:1]

    def exchange(c):
        return pltpu.make_async_remote_copy(
            src_ref=f.at[c, 1 - core], dst_ref=r1.at[c], send_sem=s1s.at[c], recv_sem=s1r.at[c],
            device_id=(i, partner), device_id_type=MESH,
        )

    def scatter(c, q, slot):
        return pltpu.make_async_remote_copy(
            src_ref=g.at[c, q], dst_ref=r2.at[c, slot], send_sem=s2s.at[c, q], recv_sem=s2r.at[c, slot],
            device_id=(i, 2 * q + core), device_id_type=MESH,
        )

    def step(t, _):
        kl = t - i * HOP
        kr = t - (n - 1 - i) * HOP
        kt = t - (n - 1) * HOP

        @pl.when((i > 0) & (kl >= 0) & (kl < pieces))
        def _():
            right(kl, sl).wait_recv()

            @pl.when(i < n - 1)
            def _():
                sl[kl] = rl[kl] + part[kl]
                right(kl, sl).start()

        @pl.when((i < n - 1) & (kr >= 0) & (kr < pieces))
        def _():
            left(kr, sr).wait_recv()

            @pl.when(i > 0)
            def _():
                sr[kr] = rr[kr] + part[kr]
                left(kr, sr).start()

        @pl.when((kt >= 0) & (kt < pieces))
        def _():
            c = lax.div(kt, blocks)
            s = lax.rem(kt, blocks)
            at = pl.ds(pl.multiple_of(s * sl_n, sl_n), sl_n)

            def finish(total):
                ids = s * sl_n + lax.broadcasted_iota(jnp.int32, (1, sl_n), 1)
                weight = jnp.where(ids < live, 1.0, 0.0).astype(jnp.float32) * scaling
                coef = (total * weight).astype(jnp.bfloat16)
                x0[c, :, at] = coef
                x1[c, :mc, at] = -coef[mc:]
                x1[c, mc:, at] = coef[:mc]

            @pl.when(i == 0)
            def _():
                finish(part[kt] + rr[kt])

            @pl.when(i == n - 1)
            def _():
                finish(part[kt] + rl[kt])

            @pl.when((i > 0) & (i < n - 1))
            def _():
                finish(part[kt] + rl[kt] + rr[kt])

            @pl.when(s == blocks - 1)
            def _():
                width = 256 if points % 256 == 0 else share
                for b in range(points // width):
                    cols = slice(b * width, (b + 1) * width)
                    acc = jnp.dot(x0[c], ebuf[0, :, cols], preferred_element_type=jnp.float32)
                    acc += jnp.dot(x1[c], ebuf[1, :, cols], preferred_element_type=jnp.float32)
                    for j in range(width // share):
                        owner = b * (width // share) + j
                        f[c, owner % 2, owner // 2] = acc[:, j * share:(j + 1) * share]
                exchange(c).start()

        kx = kt - 2

        @pl.when((kx >= 0) & (kx < pieces) & (lax.rem(kx, blocks) == blocks - 1))
        def _():
            c = lax.div(kx, blocks)
            exchange(c).wait_recv()
            for d in range(1, chips + 1):
                q = lax.rem(chip + d, chips)
                g[c, q] = f[c, core, q] + r1[c, q]
                if d < chips:
                    scatter(c, q, chip).start()
        return 0

    lax.fori_loop(0, pieces + (n - 1) * HOP + 2, step, 0)

    for c in range(chunks):
        total = g[c, chip]
        for d in range(1, chips):
            q = lax.rem(chip + d, chips)
            scatter(c, q, q).wait_recv()
            total += r2[c, q]
        fin[c * mc:(c + 1) * mc] = total[:mc]
        fin[modes + c * mc:modes + (c + 1) * mc] = total[mc:]
    out_ref[...] = fin[...].T

    def drain(k, _):
        @pl.when(i < n - 1)
        def _():
            right(k, part).wait_send()

        @pl.when(i > 0)
        def _():
            left(k, part).wait_send()
        return 0

    lax.fori_loop(0, pieces, drain, 0)
    for c in range(chunks):
        exchange(c).wait_send()
        for d in range(1, chips):
            q = lax.rem(chip + d, chips)
            scatter(c, q, chip).wait_send()


def body(n, electric, trial, counts):
    cap, points = electric.shape[1:]
    modes = trial.shape[2]
    chips = counts.shape[0] // 2
    share = points // counts.shape[0]
    chunks = 4
    blocks = 4
    pieces = chunks * blocks
    rows = 2 * modes // chunks
    piece = pltpu.VMEM((pieces, rows, cap // blocks), jnp.float32)
    dma = pltpu.SemaphoreType.DMA
    out = pl.pallas_call(
        functools.partial(kernel, n, chips, chunks, blocks),
        out_shape=jax.ShapeDtypeStruct((share, 2 * modes), jnp.float32),
        in_specs=[
            pl.BlockSpec(memory_space=pltpu.SMEM),
            pl.BlockSpec(memory_space=pltpu.VMEM),
            pl.BlockSpec(memory_space=pl.ANY),
        ],
        out_specs=pl.BlockSpec(memory_space=pltpu.VMEM),
        scratch_shapes=[
            pltpu.VMEM((2, cap, points), jnp.bfloat16),
            piece, piece, piece, piece, piece,
            pltpu.VMEM((chunks, rows, cap), jnp.bfloat16),
            pltpu.VMEM((chunks, rows, cap), jnp.bfloat16),
            pltpu.VMEM((chunks, 2, chips, rows, share), jnp.float32),
            pltpu.VMEM((chunks, chips, rows, share), jnp.float32),
            pltpu.VMEM((chunks, chips, rows, share), jnp.float32),
            pltpu.VMEM((chunks, chips, rows, share), jnp.float32),
            pltpu.VMEM((2 * modes, share), jnp.float32),
            dma((blocks, 2)),
            dma((pieces,)), dma((pieces,)), dma((pieces,)), dma((pieces,)),
            dma((chunks,)), dma((chunks,)),
            dma((chunks, chips)), dma((chunks, chips)),
        ],
        compiler_params=pltpu.CompilerParams(
            collective_id=0, has_side_effects=True, vmem_limit_bytes=60 * 1024 * 1024
        ),
    )(counts, jnp.transpose(trial, (1, 2, 0)), electric)
    return out.reshape(share, 2, modes)


def solution(mesh):
    placed = (P(None, "elec", "grid"), P("grid", None, None), P())
    return jax.shard_map(
        functools.partial(body, mesh.shape["grid"]),
        mesh=mesh, in_specs=placed, out_specs=P(("grid", "elec"), None, None), check_vma=False,
    )
```

```python
import functools

import jax
import jax.numpy as jnp
from jax import lax
from jax.experimental import pallas as pl
from jax.experimental.pallas import tpu as pltpu
from jax.sharding import PartitionSpec as P

MESH = pl.DeviceIdType.MESH
HOP = 2
LAG = 3
CHUNKS = 4
BLOCKS = 4


def kernel(
    n, chips, chunks, blocks,
    counts_ref, trial_ref, electric_ref, out_ref,
    wide, vt, ebuf, part, rl, rr, sl, sr, x0, x1, f, r1, g, r2, fin,
    esem, slsem, rlsem, srsem, rrsem, s1s, s1r, s2s, s2r,
):
    cap = ebuf.shape[1]
    points = ebuf.shape[2]
    modes = trial_ref.shape[1]
    block_chips = max(1, chips // blocks)
    mc = modes // chunks
    sl_n = cap // blocks
    pieces = chunks * blocks
    share = f.shape[-1]
    i = lax.axis_index("grid")
    e = lax.axis_index("elec")
    core = lax.rem(e, 2)
    chip = lax.div(e, 2)
    partner = e + 1 - 2 * core

    def load(s, z):
        return pltpu.make_async_copy(
            electric_ref.at[z, pl.ds(s * sl_n, sl_n), :],
            ebuf.at[z, pl.ds(s * sl_n, sl_n), :],
            esem.at[s, z],
        )

    for s in range(blocks):
        load(s, 0).start()
        load(s, 1).start()

    barrier = pltpu.get_barrier_semaphore()

    for d in (1, n - 1):
        pl.semaphore_signal(barrier, inc=1, device_id=(lax.rem(i + d, n), e), device_id_type=MESH)

    pl.semaphore_signal(barrier, inc=1, device_id=(i, partner), device_id_type=MESH)
    for d in range(1, chips):
        q = lax.rem(chip + d, chips)
        pl.semaphore_signal(barrier, inc=1, device_id=(i, 2 * q + core), device_id_type=MESH)

    def right(k, src):
        return pltpu.make_async_remote_copy(
            src_ref=src.at[k], dst_ref=rl.at[k], send_sem=slsem.at[k], recv_sem=rlsem.at[k],
            device_id=(i + 1, e), device_id_type=MESH,
        )

    def left(k, src):
        return pltpu.make_async_remote_copy(
            src_ref=src.at[k], dst_ref=rr.at[k], send_sem=srsem.at[k], recv_sem=rrsem.at[k],
            device_id=(i - 1, e), device_id_type=MESH,
        )

    def send_ends(k):
        @pl.when(i == 0)
        def _():
            right(k, part).start()

        @pl.when(i == n - 1)
        def _():
            left(k, part).start()

    wide[...] = trial_ref[...].astype(jnp.float32)
    vt[:modes] = wide[pl.ds(0, points, stride=2), :].astype(jnp.bfloat16).T
    vt[modes:] = wide[pl.ds(1, points, stride=2), :].astype(jnp.bfloat16).T

    dims = (((1,), (1,)), ((), ()))
    for s in range(blocks):
        load(s, 0).wait()
        load(s, 1).wait()
        q0 = lax.dot_general(vt[...], ebuf[0, s * sl_n:(s + 1) * sl_n, :], dims, preferred_element_type=jnp.float32)
        q1 = lax.dot_general(vt[...], ebuf[1, s * sl_n:(s + 1) * sl_n, :], dims, preferred_element_type=jnp.float32)
        real = q0[:modes] + q1[modes:]
        imag = q0[modes:] - q1[:modes]
        for c in range(chunks):
            part[c * blocks + s, :mc] = real[c * mc:(c + 1) * mc]
            part[c * blocks + s, mc:] = imag[c * mc:(c + 1) * mc]
        if s == 0:
            pl.semaphore_wait(barrier, chips + 2)
        send_ends(s)

    def rest(k, _):
        send_ends(k)
        return 0

    lax.fori_loop(blocks, pieces, rest, 0)

    live = counts_ref[e]
    total_live = lax.fori_loop(0, 2 * chips, lambda j, v: v + counts_ref[j], jnp.int32(0))
    scaling = 1.0 / jnp.sqrt(jnp.full((8, sl_n), total_live, jnp.int32).astype(jnp.float32))
    scaling = scaling[:1]

    def exchange(c, q):
        return pltpu.make_async_remote_copy(
            src_ref=f.at[c, 1 - core, q], dst_ref=r1.at[c, q], send_sem=s1s.at[c, q], recv_sem=s1r.at[c, q],
            device_id=(i, partner), device_id_type=MESH,
        )

    def scatter(c, q, slot):
        return pltpu.make_async_remote_copy(
            src_ref=g.at[c, q], dst_ref=r2.at[c, slot], send_sem=s2s.at[c, q], recv_sem=s2r.at[c, slot],
            device_id=(i, 2 * q + core), device_id_type=MESH,
        )

    def step(t, _):
        kl = t - i * HOP
        kr = t - (n - 1 - i) * HOP
        kt = t - (n - 1) * HOP

        @pl.when((i > 0) & (kl >= 0) & (kl < pieces))
        def _():
            right(kl, sl).wait_recv()

            @pl.when(i < n - 1)
            def _():
                sl[kl] = rl[kl] + part[kl]
                right(kl, sl).start()

        @pl.when((i < n - 1) & (kr >= 0) & (kr < pieces))
        def _():
            left(kr, sr).wait_recv()

            @pl.when(i > 0)
            def _():
                sr[kr] = rr[kr] + part[kr]
                left(kr, sr).start()

        @pl.when((kt >= 0) & (kt < pieces))
        def _():
            c = lax.div(kt, blocks)
            s = lax.rem(kt, blocks)
            at = pl.ds(pl.multiple_of(s * sl_n, sl_n), sl_n)

            def finish(total):
                ids = s * sl_n + lax.broadcasted_iota(jnp.int32, (1, sl_n), 1)
                weight = jnp.where(ids < live, 1.0, 0.0).astype(jnp.float32) * scaling
                coef = (total * weight).astype(jnp.bfloat16)
                x0[c, :, at] = coef
                x1[c, :mc, at] = -coef[mc:]
                x1[c, mc:, at] = coef[:mc]

            @pl.when(i == 0)
            def _():
                finish(part[kt] + rr[kt])

            @pl.when(i == n - 1)
            def _():
                finish(part[kt] + rl[kt])

            @pl.when((i > 0) & (i < n - 1))
            def _():
                finish(part[kt] + rl[kt] + rr[kt])

        kf = kt - blocks
        uf = lax.rem(kf, blocks) * block_chips

        @pl.when((kf >= 0) & (kf < pieces) & (uf < chips))
        def _():
            c = lax.div(kf, blocks)
            for j in range(block_chips):
                q = lax.rem(chip + 1 + uf + j, chips)
                cols = pl.ds(pl.multiple_of(q * 2 * share, 2 * share), 2 * share)
                acc = jnp.dot(x0[c], ebuf[0, :, cols], preferred_element_type=jnp.float32)
                acc += jnp.dot(x1[c], ebuf[1, :, cols], preferred_element_type=jnp.float32)
                f[c, 0, q] = acc[:, :share]
                f[c, 1, q] = acc[:, share:]
                exchange(c, q).start()

        kx = kf - LAG
        ux = lax.rem(kx, blocks) * block_chips

        @pl.when((kx >= 0) & (kx < pieces) & (ux < chips))
        def _():
            c = lax.div(kx, blocks)
            for j in range(block_chips):
                q = lax.rem(chip + 1 + ux + j, chips)
                exchange(c, q).wait_recv()
                g[c, q] = f[c, core, q] + r1[c, q]

                @pl.when(ux + j < chips - 1)
                def _():
                    scatter(c, q, chip).start()
        return 0

    lax.fori_loop(0, pieces + (n - 1) * HOP + blocks + LAG, step, 0)

    for c in range(chunks):
        total = g[c, chip]
        for d in range(1, chips):
            q = lax.rem(chip + d, chips)
            scatter(c, q, q).wait_recv()
            total += r2[c, q]
        fin[c * mc:(c + 1) * mc] = total[:mc]
        fin[modes + c * mc:modes + (c + 1) * mc] = total[mc:]
    out_ref[pl.ds(0, share, stride=2), :] = fin[:modes].T
    out_ref[pl.ds(1, share, stride=2), :] = fin[modes:].T

    def drain(k, _):
        @pl.when(i < n - 1)
        def _():
            right(k, part).wait_send()

        @pl.when(i > 0)
        def _():
            left(k, part).wait_send()
        return 0

    lax.fori_loop(0, pieces, drain, 0)
    for c in range(chunks):
        exchange(c, chip).wait_send()
        for d in range(1, chips):
            q = lax.rem(chip + d, chips)
            exchange(c, q).wait_send()
            scatter(c, q, chip).wait_send()


def body(n, electric, trial, counts):
    cap, points = electric.shape[1:]
    modes = trial.shape[2]
    chips = counts.shape[0] // 2
    share = points // counts.shape[0]
    chunks = CHUNKS
    blocks = BLOCKS
    pieces = chunks * blocks
    rows = 2 * modes // chunks
    piece = pltpu.VMEM((pieces, rows, cap // blocks), jnp.float32)
    dma = pltpu.SemaphoreType.DMA
    out = pl.pallas_call(
        functools.partial(kernel, n, chips, chunks, blocks),
        out_shape=jax.ShapeDtypeStruct((2 * share, modes), jnp.float32),
        in_specs=[
            pl.BlockSpec(memory_space=pltpu.SMEM),
            pl.BlockSpec(memory_space=pltpu.VMEM),
            pl.BlockSpec(memory_space=pl.ANY),
        ],
        out_specs=pl.BlockSpec(memory_space=pltpu.VMEM),
        scratch_shapes=[
            pltpu.VMEM((2 * points, modes), jnp.float32),
            pltpu.VMEM((2 * modes, points), jnp.bfloat16),
            pltpu.VMEM((2, cap, points), jnp.bfloat16),
            piece, piece, piece, piece, piece,
            pltpu.VMEM((chunks, rows, cap), jnp.bfloat16),
            pltpu.VMEM((chunks, rows, cap), jnp.bfloat16),
            pltpu.VMEM((chunks, 2, chips, rows, share), jnp.float32),
            pltpu.VMEM((chunks, chips, rows, share), jnp.float32),
            pltpu.VMEM((chunks, chips, rows, share), jnp.float32),
            pltpu.VMEM((chunks, chips, rows, share), jnp.float32),
            pltpu.VMEM((2 * modes, share), jnp.float32),
            dma((blocks, 2)),
            dma((pieces,)), dma((pieces,)), dma((pieces,)), dma((pieces,)),
            dma((chunks, chips)), dma((chunks, chips)),
            dma((chunks, chips)), dma((chunks, chips)),
        ],
        compiler_params=pltpu.CompilerParams(
            collective_id=0, has_side_effects=True, vmem_limit_bytes=60 * 1024 * 1024
        ),
    )(counts, trial.reshape(2 * points, modes), electric)
    return out.reshape(share, 2, modes)


def solution(mesh):
    placed = (P(None, "elec", "grid"), P("grid", None, None), P())
    return jax.shard_map(
        functools.partial(body, mesh.shape["grid"]),
        mesh=mesh, in_specs=placed, out_specs=P(("grid", "elec"), None, None), check_vma=False,
    )
```

```python
import functools

import jax
import jax.numpy as jnp
from jax import lax
from jax.experimental import pallas as pl
from jax.experimental.pallas import tpu as pltpu
from jax.sharding import PartitionSpec as P

MESH = pl.DeviceIdType.MESH
HOP = 3
LAG = 3
CHUNKS = 4
BLOCKS = 4


def kernel(
    n, chips, chunks, blocks,
    counts_ref, trial_ref, electric_ref, out_ref,
    held, wide, vt, ebuf, part, rl, rr, sl, sr, x0, x1, f, r1, g, r2, fin,
    tsem, esem, slsem, rlsem, srsem, rrsem, s1s, s1r, s2s, s2r,
):
    cap = ebuf.shape[1]
    points = ebuf.shape[2]
    modes = trial_ref.shape[1]
    block_chips = max(1, chips // blocks)
    mc = modes // chunks
    sl_n = cap // blocks
    pieces = chunks * blocks
    share = f.shape[-1]
    i = lax.axis_index("grid")
    e = lax.axis_index("elec")
    core = lax.rem(e, 2)
    chip = lax.div(e, 2)
    partner = e + 1 - 2 * core

    def load(s, z):
        return pltpu.make_async_copy(
            electric_ref.at[z, pl.ds(s * sl_n, sl_n), :],
            ebuf.at[z, pl.ds(s * sl_n, sl_n), :],
            esem.at[s, z],
        )

    trial_load = pltpu.make_async_copy(trial_ref, held, tsem)
    trial_load.start()
    for s in range(blocks):
        load(s, 0).start()
        load(s, 1).start()

    barrier = pltpu.get_barrier_semaphore()

    for d in (1, n - 1):
        pl.semaphore_signal(barrier, inc=1, device_id=(lax.rem(i + d, n), e), device_id_type=MESH)

    pl.semaphore_signal(barrier, inc=1, device_id=(i, partner), device_id_type=MESH)
    for d in range(1, chips):
        q = lax.rem(chip + d, chips)
        pl.semaphore_signal(barrier, inc=1, device_id=(i, 2 * q + core), device_id_type=MESH)

    def right(k, src):
        return pltpu.make_async_remote_copy(
            src_ref=src.at[k], dst_ref=rl.at[k], send_sem=slsem.at[k], recv_sem=rlsem.at[k],
            device_id=(i + 1, e), device_id_type=MESH,
        )

    def left(k, src):
        return pltpu.make_async_remote_copy(
            src_ref=src.at[k], dst_ref=rr.at[k], send_sem=srsem.at[k], recv_sem=rrsem.at[k],
            device_id=(i - 1, e), device_id_type=MESH,
        )

    def send_ends(k):
        @pl.when(i == 0)
        def _():
            right(k, part).start()

        @pl.when(i == n - 1)
        def _():
            left(k, part).start()

    trial_load.wait()
    wide[...] = held[...].astype(jnp.float32)
    vt[:modes] = wide[pl.ds(0, points, stride=2), :].astype(jnp.bfloat16).T
    vt[modes:] = wide[pl.ds(1, points, stride=2), :].astype(jnp.bfloat16).T

    dims = (((1,), (1,)), ((), ()))
    for s in range(blocks):
        load(s, 0).wait()
        load(s, 1).wait()
        q0 = lax.dot_general(vt[...], ebuf[0, s * sl_n:(s + 1) * sl_n, :], dims, preferred_element_type=jnp.float32)
        q1 = lax.dot_general(vt[...], ebuf[1, s * sl_n:(s + 1) * sl_n, :], dims, preferred_element_type=jnp.float32)
        real = q0[:modes] + q1[modes:]
        imag = q0[modes:] - q1[:modes]
        for c in range(chunks):
            part[c * blocks + s, :mc] = real[c * mc:(c + 1) * mc]
            part[c * blocks + s, mc:] = imag[c * mc:(c + 1) * mc]
        if s == 0:
            pl.semaphore_wait(barrier, chips + 2)
        send_ends(s)

    def rest(k, _):
        send_ends(k)
        return 0

    lax.fori_loop(blocks, pieces, rest, 0)

    live = counts_ref[e]
    total_live = lax.fori_loop(0, 2 * chips, lambda j, v: v + counts_ref[j], jnp.int32(0))
    scaling = 1.0 / jnp.sqrt(jnp.full((8, sl_n), total_live, jnp.int32).astype(jnp.float32))
    scaling = scaling[:1]

    def exchange(c, q):
        return pltpu.make_async_remote_copy(
            src_ref=f.at[c, 1 - core, q], dst_ref=r1.at[c, q], send_sem=s1s.at[c, q], recv_sem=s1r.at[c, q],
            device_id=(i, partner), device_id_type=MESH,
        )

    def scatter(c, q, slot):
        return pltpu.make_async_remote_copy(
            src_ref=g.at[c, q], dst_ref=r2.at[c, slot], send_sem=s2s.at[c, q], recv_sem=s2r.at[c, slot],
            device_id=(i, 2 * q + core), device_id_type=MESH,
        )

    def step(t, _):
        kl = t - i * HOP
        kr = t - (n - 1 - i) * HOP
        kt = t - (n - 1) * HOP

        @pl.when((i > 0) & (kl >= 0) & (kl < pieces))
        def _():
            right(kl, sl).wait_recv()

            @pl.when(i < n - 1)
            def _():
                sl[kl] = rl[kl] + part[kl]
                right(kl, sl).start()

        @pl.when((i < n - 1) & (kr >= 0) & (kr < pieces))
        def _():
            left(kr, sr).wait_recv()

            @pl.when(i > 0)
            def _():
                sr[kr] = rr[kr] + part[kr]
                left(kr, sr).start()

        @pl.when((kt >= 0) & (kt < pieces))
        def _():
            c = lax.div(kt, blocks)
            s = lax.rem(kt, blocks)
            at = pl.ds(pl.multiple_of(s * sl_n, sl_n), sl_n)

            def finish(total):
                ids = s * sl_n + lax.broadcasted_iota(jnp.int32, (1, sl_n), 1)
                weight = jnp.where(ids < live, 1.0, 0.0).astype(jnp.float32) * scaling
                coef = (total * weight).astype(jnp.bfloat16)
                x0[c, :, at] = coef
                x1[c, :mc, at] = -coef[mc:]
                x1[c, mc:, at] = coef[:mc]

            @pl.when(i == 0)
            def _():
                finish(part[kt] + rr[kt])

            @pl.when(i == n - 1)
            def _():
                finish(part[kt] + rl[kt])

            @pl.when((i > 0) & (i < n - 1))
            def _():
                finish(part[kt] + rl[kt] + rr[kt])

        kf = kt - blocks
        uf = lax.rem(kf, blocks) * block_chips

        @pl.when((kf >= 0) & (kf < pieces) & (uf < chips))
        def _():
            c = lax.div(kf, blocks)
            for j in range(block_chips):
                q = lax.rem(chip + 1 + uf + j, chips)
                cols = pl.ds(pl.multiple_of(q * 2 * share, 2 * share), 2 * share)
                acc = jnp.dot(x0[c], ebuf[0, :, cols], preferred_element_type=jnp.float32)
                acc += jnp.dot(x1[c], ebuf[1, :, cols], preferred_element_type=jnp.float32)
                f[c, 0, q] = acc[:, :share]
                f[c, 1, q] = acc[:, share:]
                exchange(c, q).start()

        kx = kf - LAG
        ux = lax.rem(kx, blocks) * block_chips

        @pl.when((kx >= 0) & (kx < pieces) & (ux < chips))
        def _():
            c = lax.div(kx, blocks)
            for j in range(block_chips):
                q = lax.rem(chip + 1 + ux + j, chips)
                exchange(c, q).wait_recv()
                g[c, q] = f[c, core, q] + r1[c, q]

                @pl.when(ux + j < chips - 1)
                def _():
                    scatter(c, q, chip).start()
        return 0

    lax.fori_loop(0, pieces + (n - 1) * HOP + blocks + LAG, step, 0)

    for c in range(chunks):
        total = g[c, chip]
        for d in range(1, chips):
            q = lax.rem(chip + d, chips)
            scatter(c, q, q).wait_recv()
            total += r2[c, q]
        fin[c * mc:(c + 1) * mc] = total[:mc]
        fin[modes + c * mc:modes + (c + 1) * mc] = total[mc:]
    out_ref[pl.ds(0, share, stride=2), :] = fin[:modes].T
    out_ref[pl.ds(1, share, stride=2), :] = fin[modes:].T

    def drain(k, _):
        @pl.when(i < n - 1)
        def _():
            right(k, part).wait_send()

        @pl.when(i > 0)
        def _():
            left(k, part).wait_send()
        return 0

    lax.fori_loop(0, pieces, drain, 0)
    for c in range(chunks):
        exchange(c, chip).wait_send()
        for d in range(1, chips):
            q = lax.rem(chip + d, chips)
            exchange(c, q).wait_send()
            scatter(c, q, chip).wait_send()


def body(n, electric, trial, counts):
    cap, points = electric.shape[1:]
    modes = trial.shape[2]
    chips = counts.shape[0] // 2
    share = points // counts.shape[0]
    chunks = CHUNKS
    blocks = BLOCKS
    pieces = chunks * blocks
    rows = 2 * modes // chunks
    piece = pltpu.VMEM((pieces, rows, cap // blocks), jnp.float32)
    dma = pltpu.SemaphoreType.DMA
    out = pl.pallas_call(
        functools.partial(kernel, n, chips, chunks, blocks),
        out_shape=jax.ShapeDtypeStruct((2 * share, modes), jnp.float32),
        in_specs=[
            pl.BlockSpec(memory_space=pltpu.SMEM),
            pl.BlockSpec(memory_space=pl.ANY),
            pl.BlockSpec(memory_space=pl.ANY),
        ],
        out_specs=pl.BlockSpec(memory_space=pltpu.VMEM),
        scratch_shapes=[
            pltpu.VMEM((2 * points, modes), jnp.bfloat16),
            pltpu.VMEM((2 * points, modes), jnp.float32),
            pltpu.VMEM((2 * modes, points), jnp.bfloat16),
            pltpu.VMEM((2, cap, points), jnp.bfloat16),
            piece, piece, piece, piece, piece,
            pltpu.VMEM((chunks, rows, cap), jnp.bfloat16),
            pltpu.VMEM((chunks, rows, cap), jnp.bfloat16),
            pltpu.VMEM((chunks, 2, chips, rows, share), jnp.float32),
            pltpu.VMEM((chunks, chips, rows, share), jnp.float32),
            pltpu.VMEM((chunks, chips, rows, share), jnp.float32),
            pltpu.VMEM((chunks, chips, rows, share), jnp.float32),
            pltpu.VMEM((2 * modes, share), jnp.float32),
            dma(()), dma((blocks, 2)),
            dma((pieces,)), dma((pieces,)), dma((pieces,)), dma((pieces,)),
            dma((chunks, chips)), dma((chunks, chips)),
            dma((chunks, chips)), dma((chunks, chips)),
        ],
        compiler_params=pltpu.CompilerParams(
            collective_id=0, has_side_effects=True, vmem_limit_bytes=60 * 1024 * 1024
        ),
    )(counts, trial.reshape(2 * points, modes), electric)
    return out.reshape(share, 2, modes)


def solution(mesh):
    placed = (P(None, "elec", "grid"), P("grid", None, None), P())
    return jax.shard_map(
        functools.partial(body, mesh.shape["grid"]),
        mesh=mesh, in_specs=placed, out_specs=P(("grid", "elec"), None, None), check_vma=False,
    )
```

```python
import functools

import jax
import jax.numpy as jnp
from jax import lax
from jax.experimental import pallas as pl
from jax.experimental.pallas import tpu as pltpu
from jax.sharding import PartitionSpec as P

MESH = pl.DeviceIdType.MESH
HOP = 3
LAG = 3
CHUNKS = 4
BLOCKS = 4


def kernel(
    n, chips, chunks, blocks,
    counts_ref, trial_ref, electric_ref, out_ref,
    wide, vt, ebuf, part, rl, rr, sl, sr, x0, x1, f, r1, g, r2, fin,
    esem, slsem, rlsem, srsem, rrsem, s1s, s1r, s2s, s2r,
):
    cap = ebuf.shape[1]
    points = ebuf.shape[2]
    modes = trial_ref.shape[1]
    block_chips = max(1, chips // blocks)
    mc = modes // chunks
    sl_n = cap // blocks
    pieces = chunks * blocks
    share = f.shape[-1]
    i = lax.axis_index("grid")
    e = lax.axis_index("elec")
    core = lax.rem(e, 2)
    chip = lax.div(e, 2)
    partner = e + 1 - 2 * core

    def load(s, z):
        return pltpu.make_async_copy(
            electric_ref.at[z, pl.ds(s * sl_n, sl_n), :],
            ebuf.at[z, pl.ds(s * sl_n, sl_n), :],
            esem.at[s, z],
        )

    for s in range(blocks):
        load(s, 0).start()
        load(s, 1).start()

    barrier = pltpu.get_barrier_semaphore()

    for d in (1, n - 1):
        pl.semaphore_signal(barrier, inc=1, device_id=(lax.rem(i + d, n), e), device_id_type=MESH)

    pl.semaphore_signal(barrier, inc=1, device_id=(i, partner), device_id_type=MESH)
    for d in range(1, chips):
        q = lax.rem(chip + d, chips)
        pl.semaphore_signal(barrier, inc=1, device_id=(i, 2 * q + core), device_id_type=MESH)

    def right(k, src):
        return pltpu.make_async_remote_copy(
            src_ref=src.at[k], dst_ref=rl.at[k], send_sem=slsem.at[k], recv_sem=rlsem.at[k],
            device_id=(i + 1, e), device_id_type=MESH,
        )

    def left(k, src):
        return pltpu.make_async_remote_copy(
            src_ref=src.at[k], dst_ref=rr.at[k], send_sem=srsem.at[k], recv_sem=rrsem.at[k],
            device_id=(i - 1, e), device_id_type=MESH,
        )

    def send_ends(k):
        @pl.when(i == 0)
        def _():
            right(k, part).start()

        @pl.when(i == n - 1)
        def _():
            left(k, part).start()

    wide[...] = trial_ref[...].astype(jnp.float32)
    vt[:modes] = wide[pl.ds(0, points, stride=2), :].astype(jnp.bfloat16).T
    vt[modes:] = wide[pl.ds(1, points, stride=2), :].astype(jnp.bfloat16).T

    dims = (((1,), (1,)), ((), ()))
    for s in range(blocks):
        load(s, 0).wait()
        load(s, 1).wait()
        q0 = lax.dot_general(vt[...], ebuf[0, s * sl_n:(s + 1) * sl_n, :], dims, preferred_element_type=jnp.float32)
        q1 = lax.dot_general(vt[...], ebuf[1, s * sl_n:(s + 1) * sl_n, :], dims, preferred_element_type=jnp.float32)
        real = q0[:modes] + q1[modes:]
        imag = q0[modes:] - q1[:modes]
        for c in range(chunks):
            part[c * blocks + s, :mc] = real[c * mc:(c + 1) * mc]
            part[c * blocks + s, mc:] = imag[c * mc:(c + 1) * mc]
        if s == 0:
            pl.semaphore_wait(barrier, chips + 2)
        send_ends(s)

    def rest(k, _):
        send_ends(k)
        return 0

    lax.fori_loop(blocks, pieces, rest, 0)

    live = counts_ref[e]
    total_live = lax.fori_loop(0, 2 * chips, lambda j, v: v + counts_ref[j], jnp.int32(0))
    scaling = 1.0 / jnp.sqrt(jnp.full((8, sl_n), total_live, jnp.int32).astype(jnp.float32))
    scaling = scaling[:1]

    def exchange(c, q):
        return pltpu.make_async_remote_copy(
            src_ref=f.at[c, 1 - core, q], dst_ref=r1.at[c, q], send_sem=s1s.at[c, q], recv_sem=s1r.at[c, q],
            device_id=(i, partner), device_id_type=MESH,
        )

    def scatter(c, q, slot):
        return pltpu.make_async_remote_copy(
            src_ref=g.at[c, q], dst_ref=r2.at[c, slot], send_sem=s2s.at[c, q], recv_sem=s2r.at[c, slot],
            device_id=(i, 2 * q + core), device_id_type=MESH,
        )

    def step(t, _):
        kl = t - i * HOP
        kr = t - (n - 1 - i) * HOP
        kt = t - (n - 1) * HOP

        @pl.when((i > 0) & (kl >= 0) & (kl < pieces))
        def _():
            right(kl, sl).wait_recv()

            @pl.when(i < n - 1)
            def _():
                sl[kl] = rl[kl] + part[kl]
                right(kl, sl).start()

        @pl.when((i < n - 1) & (kr >= 0) & (kr < pieces))
        def _():
            left(kr, sr).wait_recv()

            @pl.when(i > 0)
            def _():
                sr[kr] = rr[kr] + part[kr]
                left(kr, sr).start()

        @pl.when((kt >= 0) & (kt < pieces))
        def _():
            c = lax.div(kt, blocks)
            s = lax.rem(kt, blocks)
            at = pl.ds(pl.multiple_of(s * sl_n, sl_n), sl_n)

            def finish(total):
                ids = s * sl_n + lax.broadcasted_iota(jnp.int32, (1, sl_n), 1)
                weight = jnp.where(ids < live, 1.0, 0.0).astype(jnp.float32) * scaling
                coef = (total * weight).astype(jnp.bfloat16)
                x0[c, :, at] = coef
                x1[c, :mc, at] = -coef[mc:]
                x1[c, mc:, at] = coef[:mc]

            @pl.when(i == 0)
            def _():
                finish(part[kt] + rr[kt])

            @pl.when(i == n - 1)
            def _():
                finish(part[kt] + rl[kt])

            @pl.when((i > 0) & (i < n - 1))
            def _():
                finish(part[kt] + rl[kt] + rr[kt])

        kf = kt - blocks
        uf = lax.rem(kf, blocks) * block_chips

        @pl.when((kf >= 0) & (kf < pieces) & (uf < chips))
        def _():
            c = lax.div(kf, blocks)
            for j in range(block_chips):
                q = lax.rem(chip + 1 + uf + j, chips)
                cols = pl.ds(pl.multiple_of(q * 2 * share, 2 * share), 2 * share)
                acc = jnp.dot(x0[c], ebuf[0, :, cols], preferred_element_type=jnp.float32)
                acc += jnp.dot(x1[c], ebuf[1, :, cols], preferred_element_type=jnp.float32)
                f[c, 0, q] = acc[:, :share]
                f[c, 1, q] = acc[:, share:]
                exchange(c, q).start()

        kx = kf - LAG
        ux = lax.rem(kx, blocks) * block_chips

        @pl.when((kx >= 0) & (kx < pieces) & (ux < chips))
        def _():
            c = lax.div(kx, blocks)
            for j in range(block_chips):
                q = lax.rem(chip + 1 + ux + j, chips)
                exchange(c, q).wait_recv()
                g[c, q] = f[c, core, q] + r1[c, q]

                @pl.when(ux + j < chips - 1)
                def _():
                    scatter(c, q, chip).start()
        return 0

    lax.fori_loop(0, pieces + (n - 1) * HOP + blocks + LAG, step, 0)

    for c in range(chunks):
        total = g[c, chip]
        for d in range(1, chips):
            q = lax.rem(chip + d, chips)
            scatter(c, q, q).wait_recv()
            total += r2[c, q]
        fin[c * mc:(c + 1) * mc] = total[:mc]
        fin[modes + c * mc:modes + (c + 1) * mc] = total[mc:]
    out_ref[pl.ds(0, share, stride=2), :] = fin[:modes].T
    out_ref[pl.ds(1, share, stride=2), :] = fin[modes:].T

    def drain(k, _):
        @pl.when(i < n - 1)
        def _():
            right(k, part).wait_send()

        @pl.when(i > 0)
        def _():
            left(k, part).wait_send()
        return 0

    lax.fori_loop(0, pieces, drain, 0)
    for c in range(chunks):
        exchange(c, chip).wait_send()
        for d in range(1, chips):
            q = lax.rem(chip + d, chips)
            exchange(c, q).wait_send()
            scatter(c, q, chip).wait_send()


def body(n, electric, trial, counts):
    cap, points = electric.shape[1:]
    modes = trial.shape[2]
    chips = counts.shape[0] // 2
    share = points // counts.shape[0]
    chunks = CHUNKS
    blocks = BLOCKS
    pieces = chunks * blocks
    rows = 2 * modes // chunks
    piece = pltpu.VMEM((pieces, rows, cap // blocks), jnp.float32)
    dma = pltpu.SemaphoreType.DMA
    out = pl.pallas_call(
        functools.partial(kernel, n, chips, chunks, blocks),
        out_shape=jax.ShapeDtypeStruct((2 * share, modes), jnp.float32),
        in_specs=[
            pl.BlockSpec(memory_space=pltpu.SMEM),
            pl.BlockSpec(memory_space=pltpu.VMEM),
            pl.BlockSpec(memory_space=pl.ANY),
        ],
        out_specs=pl.BlockSpec(memory_space=pltpu.VMEM),
        scratch_shapes=[
            pltpu.VMEM((2 * points, modes), jnp.float32),
            pltpu.VMEM((2 * modes, points), jnp.bfloat16),
            pltpu.VMEM((2, cap, points), jnp.bfloat16),
            piece, piece, piece, piece, piece,
            pltpu.VMEM((chunks, rows, cap), jnp.bfloat16),
            pltpu.VMEM((chunks, rows, cap), jnp.bfloat16),
            pltpu.VMEM((chunks, 2, chips, rows, share), jnp.float32),
            pltpu.VMEM((chunks, chips, rows, share), jnp.float32),
            pltpu.VMEM((chunks, chips, rows, share), jnp.float32),
            pltpu.VMEM((chunks, chips, rows, share), jnp.float32),
            pltpu.VMEM((2 * modes, share), jnp.float32),
            dma((blocks, 2)),
            dma((pieces,)), dma((pieces,)), dma((pieces,)), dma((pieces,)),
            dma((chunks, chips)), dma((chunks, chips)),
            dma((chunks, chips)), dma((chunks, chips)),
        ],
        compiler_params=pltpu.CompilerParams(
            collective_id=0, has_side_effects=True, vmem_limit_bytes=60 * 1024 * 1024
        ),
    )(counts, trial.reshape(2 * points, modes), electric)
    return out.reshape(share, 2, modes)


def solution(mesh):
    placed = (P(None, "elec", "grid"), P("grid", None, None), P())
    return jax.shard_map(
        functools.partial(body, mesh.shape["grid"]),
        mesh=mesh, in_specs=placed, out_specs=P(("grid", "elec"), None, None), check_vma=False,
    )
```
